32 devices in a mesh: shard: 4 (over y, x), mp: 4 (over z), segment: 2 (over core).
Axes of the slice: x: 2, y: 2, z: 4, core: 2. Of those that a mesh axis runs over, the one named last changes fastest.
Arguments:
- store_tokens: int32 [256, 48], P('shard'), may hold values from 0 to 16383
- retrieved: int32 [4, 12], replicated, may hold values from 0 to 63
- owner_shard: int32 [48, 1], replicated, may hold values from 0 to 3; in each aligned block of 12 rows (0 to 11, 12 to 23, ...) at most 3 rows name the same one
- targets: int32 [4, 64], P('shard'), may hold values from 0 to 16383
- vocab_table: bfloat16 [16384, 4096], P(None, ('mp', 'segment')), may hold values from -6 to 6
- norm_gains: float32 [3, 4096], replicated, may hold values from 0.1 to 1.9
- layer_weights: bfloat16 [2, 4, 4096, 4096], P('segment', None, 'shard', 'mp'), may hold values from -0.09375 to 0.09375
Outputs:
- encoded: bfloat16 [2304, 4096], P('shard', ('mp', 'segment'))
- decoded: bfloat16 [256, 4096], P('shard', ('mp', 'segment'))
The draws below stay inside these ranges and needn't reach their ends.
Inputs may be any that keep to these rules, and one draw needn't show every extreme that they name: `owner_shard`: within the 12 passages of one question no shard owns more than 3; in every draw some question has exactly 3 passages from one shard.
All inputs are finite; a program needn't handle non-finite values.
Results may differ from the reference program's by a relative error of at most 0.015.
Values may be sent and summed in bfloat16 or wider, within the bound.
A program may use at most 128 MiB of HBM per device.

```python
import math
import jax
import jax.numpy as jnp
import numpy as np
from jax import lax

D = 4096
HEADS = 64
DH = 64
V = 16384
L = 48
PASS_DEV = 12
STORE = 64
TGT = 64
CAP = 3
INNER = 4096
QUESTIONS = 4
N_SHARD = 4
N_MP = 4


def set_ends(result, rng, low, high):
    dims = result.shape
    spot = [jax.random.randint(jax.random.fold_in(rng, axis), (), 0, dims[axis]) for axis in range(len(dims))]
    result = result.at[tuple(spot)].set(low)
    longest = dims.index(max(dims))
    spot[longest] = (spot[longest] + 1) % dims[longest]
    return result.at[tuple(spot)].set(high)


def levels(key, shape, split, least, largest):
    level, own = 1.0, jax.random.fold_in(key, 6)
    for axis_at, parts in split:
        steps = jnp.exp(jax.random.uniform(jax.random.fold_in(own, axis_at), (parts,), jnp.float32, least / len(split), largest / len(split)))
        level = level * jnp.repeat(steps, shape[axis_at] // parts).reshape([-1 if axis == axis_at else 1 for axis in range(len(shape))])
    return level


def rank_table(number_of, lean):
    weights = [(1 << 20) // math.isqrt(standing ** lean) + 1 for standing in range(1, number_of + 1)]
    spread = 1 + sum(weights) // (1 << 30)
    return np.cumsum(np.array([max(1, weight // spread) for weight in weights]))


def ranked(stream_key, extent, number_of, slope):
    grid = rank_table(number_of, slope)
    pick = jax.random.randint(jax.random.fold_in(stream_key, 1), extent, 0, int(grid[number_of - 1]))
    grade = jnp.searchsorted(jnp.asarray(grid, jnp.int32), pick, side="right")
    return jax.random.permutation(jax.random.fold_in(stream_key, 2), number_of)[grade].astype(jnp.int32)


def assign_block(own_key, own, number, rows, count, top, limit, skew):
    sequence = jax.random.permutation(own_key, count)
    packed, usual = load_shares(count, rows * top, limit, skew, True), load_shares(count, rows * top, limit, skew, False)
    places = jnp.arange(count)

    def named(sizes, turn):
        used = int((sizes > 0).sum())
        fixed = max(1, used // 4)
        moved = fixed + (places - fixed + turn * (used - fixed)) % max(1, count - fixed)
        return jnp.zeros((count,), jnp.int32).at[sequence[jnp.where(places < fixed, places, moved)]].set(jnp.asarray(sizes, jnp.int32))

    sizes = jnp.where(number % 4 == 0, named(packed, number // 4), named(usual, number - number // 4 - 1))
    mixed = jax.random.permutation(jax.random.fold_in(own, 3), count)
    donor, receiver = mixed[0:count // 2 * 2:2], mixed[1:count // 2 * 2:2]
    room = jnp.minimum(sizes[donor] - 1, limit - sizes[receiver]) // 2
    room = jnp.where((donor == sequence[0]) | (receiver == sequence[0]) | (sizes[receiver] == 0), 0, jnp.maximum(room, 0))
    moved = jax.random.randint(jax.random.fold_in(own, 4), (count // 2,), 0, 1 << 20) % (room + 1)
    sizes = sizes.at[donor].add(-moved).at[receiver].add(moved)
    members = jnp.searchsorted(jnp.cumsum(sizes), jnp.arange(rows * top), side="right").astype(jnp.int32)
    table = members.reshape(top, rows).T
    table = table[jax.random.permutation(jax.random.fold_in(own, 1), rows)]
    turn = jax.random.randint(jax.random.fold_in(own, 2), (rows, 1), 0, top)
    return jnp.take_along_axis(table, (jnp.arange(top)[None, :] + turn) % top, axis=1)


def load_shares(amount, total, reach, lean, full):
    loads = [(1 << 20) // math.isqrt(standing ** lean) + 1 for standing in range(1, amount + 1)]
    largest = reach if full else min(reach, max(-(-total // amount), total * loads[0] // sum(loads)))
    least = 1 if total - largest >= amount - 1 else 0
    given, surplus = [largest] + [least] * (amount - 1), total - largest - least * (amount - 1)
    while surplus > 0:
        candidates = [i for i in range(1, amount) if given[i] < largest] or [i for i in range(1, amount) if given[i] < reach]
        pool, budget = sum([loads[i] for i in candidates]), surplus
        for i in candidates:
            extra = min(reach - given[i], max(1, budget * loads[i] // pool), surplus)
            given[i] = given[i] + extra
            surplus = surplus - extra
    return np.array(given)


def scatter_about(stream_key, shape, width, bound, cuts=(), kind=jnp.bfloat16):
    loudness = levels(stream_key, shape, cuts, -0.22, 0.18) if cuts else 1.0
    result = jax.random.normal(stream_key, shape, jnp.float32) * width * loudness
    return jnp.minimum(jnp.maximum(result, -bound), bound).astype(kind)


def setup_inputs(seed: int = 0) -> dict:
    streams_of = jax.random.split(jax.random.key(seed), 8)
    store_tokens = set_ends(ranked(streams_of[0], (STORE * N_SHARD, L), V, 2), jax.random.fold_in(streams_of[0], 3), 0, V - 1).astype(jnp.int32)
    retrieved = set_ends(jax.random.randint(streams_of[1], (QUESTIONS, PASS_DEV), 0, STORE), jax.random.fold_in(streams_of[1], 1), 0, STORE - 1).astype(jnp.int32)
    owner_shard_keys = jax.random.split(jax.random.fold_in(streams_of[2], 1), (QUESTIONS * PASS_DEV) // PASS_DEV)
    owner_shard_turns = jax.random.permutation(jax.random.fold_in(streams_of[2], 3), (QUESTIONS * PASS_DEV) // PASS_DEV)
    owner_shard = jax.vmap(lambda own, number: assign_block(jax.random.fold_in(streams_of[2], 2), own, number, PASS_DEV, QUESTIONS, 1, CAP, 2))(owner_shard_keys, owner_shard_turns).reshape((QUESTIONS * PASS_DEV, 1))
    targets = set_ends(ranked(streams_of[3], (QUESTIONS, TGT), V, 2), jax.random.fold_in(streams_of[3], 3), 0, V - 1).astype(jnp.int32)
    vocab_table = scatter_about(streams_of[4], (V, D), 1.0, 6.0, ((1, 8),))
    norm_gains = jnp.clip(1.0 + 0.18 * jax.random.normal(streams_of[5], (3, D), jnp.float32), 0.1, 1.9)
    layer_weights = scatter_about(streams_of[6], (2, 4, D, INNER), D ** -0.5, 0.09375, ((0, 2), (2, 4), (3, 4)))
    return {"store_tokens": store_tokens, "retrieved": retrieved, "owner_shard": owner_shard, "targets": targets, "vocab_table": vocab_table, "norm_gains": norm_gains, "layer_weights": layer_weights}


epsilon = 1e-06

def rms_scale(rows_f32):
    return lax.rsqrt(lax.optimization_barrier(jnp.mean(rows_f32 * rows_f32, axis=-1)) + epsilon)

def attend(query_rows, key_rows, value_rows):
    batch_size = query_rows.shape[0]
    query_heads = query_rows.astype(jnp.float32).reshape(batch_size, query_rows.shape[1], HEADS, DH)
    key_heads = key_rows.astype(jnp.float32).reshape(batch_size, key_rows.shape[1], HEADS, DH)
    value_heads = value_rows.astype(jnp.float32).reshape(batch_size, value_rows.shape[1], HEADS, DH)
    scores = jnp.einsum('brhd,bshd->bhrs', query_heads, key_heads) * DH ** (-0.5)
    shifted = jnp.exp(scores - lax.optimization_barrier(jnp.max(scores, axis=-1, keepdims=True)))
    attention = (shifted / lax.optimization_barrier(jnp.sum(shifted, axis=-1, keepdims=True))).astype(jnp.bfloat16)
    mixture = jnp.einsum('bhrs,bshd->brhd', attention.astype(jnp.float32), value_heads)
    return mixture.astype(jnp.bfloat16).reshape(batch_size * query_rows.shape[1], HEADS * DH)

def out_project(context, out_weight):
    group_width = HEADS * DH // N_MP
    summed = jnp.zeros((context.shape[0], out_weight.shape[0]), jnp.float32)
    for group_index in range(N_MP):
        low = group_index * group_width
        partial_value = jnp.dot(context[:, low:low + group_width], out_weight[:, low:low + group_width].T, preferred_element_type=jnp.float32)
        rounded = lax.optimization_barrier(partial_value.astype(jnp.bfloat16))
        summed = summed + rounded.astype(jnp.float32)
    return summed

def project_rows(rows, gain, weight):
    rows_f32 = rows.astype(jnp.float32)
    scaled = (rows_f32 * gain).astype(jnp.bfloat16)
    product = jnp.dot(scaled, weight, preferred_element_type=jnp.float32)
    return (product * rms_scale(rows_f32)[:, None]).astype(jnp.bfloat16)

def reference(store_tokens, retrieved, owner_shard, targets, vocab_table, norm_gains, layer_weights):
    owners = owner_shard.reshape(QUESTIONS, PASS_DEV)
    store_rows = (owners * STORE + retrieved).reshape(-1).astype(jnp.int32)
    passage_ids = jnp.take(store_tokens, store_rows, axis=0).reshape(-1)
    embedded = jnp.take(vocab_table, passage_ids, axis=0)
    enc_q = project_rows(embedded, norm_gains[0], layer_weights[0, 0])
    enc_k = project_rows(embedded, norm_gains[0], layer_weights[0, 1])
    enc_v = project_rows(embedded, norm_gains[0], layer_weights[0, 2])
    passage_shape = (QUESTIONS * PASS_DEV, L, HEADS * DH)
    enc_context = attend(enc_q.reshape(passage_shape), enc_k.reshape(passage_shape), enc_v.reshape(passage_shape))
    encoded = (embedded.astype(jnp.float32) + out_project(enc_context, layer_weights[0, 3])).astype(jnp.bfloat16)
    target_rows = jnp.take(vocab_table, targets.reshape(-1), axis=0)
    dec_q = project_rows(target_rows, norm_gains[1], layer_weights[1, 0])
    cross_k = project_rows(encoded, norm_gains[2], layer_weights[1, 1])
    cross_v = project_rows(encoded, norm_gains[2], layer_weights[1, 2])
    joined_shape = (QUESTIONS, PASS_DEV * L, HEADS * DH)
    dec_context = attend(dec_q.reshape(QUESTIONS, TGT, HEADS * DH), cross_k.reshape(joined_shape), cross_v.reshape(joined_shape))
    decoded = (target_rows.astype(jnp.float32) + out_project(dec_context, layer_weights[1, 3])).astype(jnp.bfloat16)
    return (encoded, decoded)
```

```python
import jax
import jax.numpy as jnp
from jax import lax
from jax.sharding import PartitionSpec as P

D = 4096
DH = 64


epsilon = 1e-06


def attend(query_rows, key_rows, value_rows, head_count):
    batch_size = query_rows.shape[0]
    head_size = query_rows.shape[2] // head_count
    query_heads = query_rows.reshape(batch_size, query_rows.shape[1], head_count, head_size)
    key_heads = key_rows.reshape(batch_size, key_rows.shape[1], head_count, head_size)
    value_heads = value_rows.reshape(batch_size, value_rows.shape[1], head_count, head_size)
    scores = jnp.einsum(
        "brhd,bshd->bhrs", query_heads, key_heads, preferred_element_type=jnp.float32
    ) * head_size ** (-0.5)
    shifted = jnp.exp(scores - jnp.max(scores, axis=-1, keepdims=True))
    attention = (shifted / jnp.sum(shifted, axis=-1, keepdims=True)).astype(jnp.bfloat16)
    mixture = jnp.einsum(
        "bhrs,bshd->brhd", attention, value_heads, preferred_element_type=jnp.float32
    )
    return mixture.astype(jnp.bfloat16).reshape(
        batch_size * query_rows.shape[1], head_count * head_size
    )


def swap_segments(block):
    segments = lax.axis_size("segment")
    me = lax.axis_index("segment")
    half = block.shape[3] // segments
    kept = lax.dynamic_slice_in_dim(block[0], me * half, half, axis=2)
    sent = lax.dynamic_slice_in_dim(block[0], (1 - me) * half, half, axis=2)
    other = lax.ppermute(sent, "segment", [(0, 1), (1, 0)])
    return jnp.where(me == 0, kept, other), jnp.where(me == 0, other, kept)


def shard_pieces(block):
    count = lax.axis_size("shard")
    me = lax.axis_index("shard")
    rows = block.shape[1]
    if count != 4:
        whole = lax.all_gather(block, "shard", axis=1, tiled=True)
        return [(i, 0, whole[:, i * rows : (i + 1) * rows]) for i in range(count)]
    across_x = [(i, i ^ 1) for i in range(4)]
    across_y = [(i, i ^ 2) for i in range(4)]
    from_x = lax.ppermute(block, "shard", across_x)
    from_y = lax.ppermute(block, "shard", across_y)
    top = lax.ppermute(from_y[:, : rows // 2], "shard", across_x)
    bottom = lax.ppermute(from_x[:, rows // 2 :], "shard", across_y)
    return [
        (me, 0, block),
        (me ^ 1, 0, from_x),
        (me ^ 2, 0, from_y),
        (me ^ 3, 0, top),
        (me ^ 3, rows // 2, bottom),
    ]


def after(value, pieces):
    return lax.optimization_barrier((value, pieces[-1][2], pieces[-2][2]))[0]


def project(rows_in, pieces, shard_rows):
    total = None
    for owner, first, block in pieces:
        depth = block.shape[1]
        part = lax.dynamic_slice_in_dim(rows_in, owner * shard_rows + first, depth, axis=1)
        term = jnp.einsum("rn,knh->rkh", part, block, preferred_element_type=jnp.float32)
        total = term if total is None else total + term
    return total


def in_order(pieces, shard_rows):
    columns = pieces[0][2].shape[2]
    whole = jnp.zeros((D, columns), jnp.bfloat16)
    for owner, first, block in pieces:
        whole = lax.dynamic_update_slice_in_dim(
            whole, block[0], owner * shard_rows + first, axis=0
        )
    return whole


def body(store_tokens, retrieved, owner_shard, targets, vocab_table, norm_gains, layer_weights):
    shard_count = lax.axis_size("shard")
    my_shard = lax.axis_index("shard")
    per_question = retrieved.shape[1]
    length = store_tokens.shape[1]
    slot_cap = max(2, (per_question + shard_count - 1) // shard_count)
    owners = owner_shard.reshape(retrieved.shape)
    positions = jnp.arange(per_question)
    before = positions[None, :] < positions[:, None]
    matches = owners[:, :, None] == owners[:, None, :]
    slot_rank = jnp.sum(jnp.where(matches & before[None], 1, 0), axis=2).astype(jnp.int32)
    slot_numbers = jnp.arange(slot_cap)
    chosen = (owners[:, None, :] == my_shard) & (
        slot_rank[:, None, :] == slot_numbers[None, :, None]
    )
    local_rows = jnp.sum(jnp.where(chosen, retrieved[:, None, :], 0), axis=2)
    send_ids = jnp.take(store_tokens, local_rows.reshape(-1), axis=0).reshape(
        shard_count, slot_cap, length
    )
    arrived = lax.all_to_all(send_ids, "shard", split_axis=0, concat_axis=0, tiled=True)
    mine_owner = lax.dynamic_index_in_dim(owners, my_shard, 0, keepdims=False)
    mine_rank = lax.dynamic_index_in_dim(slot_rank, my_shard, 0, keepdims=False)
    arrived_rows = arrived.reshape(shard_count * slot_cap, length)
    passage_ids = jnp.take(arrived_rows, mine_owner * slot_cap + mine_rank, axis=0).reshape(-1)
    enc_qkv, dec_qkv = swap_segments(layer_weights[:, 0:3])
    enc_out, dec_out = swap_segments(layer_weights[:, 3:4])
    shard_rows = layer_weights.shape[2]
    enc_pieces = shard_pieces(enc_qkv)
    enc_out_pieces = shard_pieces(after(enc_out, enc_pieces))
    dec_pieces = shard_pieces(after(dec_qkv, enc_out_pieces))
    dec_out_pieces = shard_pieces(after(dec_out, dec_pieces))
    head_block = enc_qkv.shape[2]
    head_count = head_block // DH
    pass_rows = passage_ids.shape[0]
    all_ids = jnp.concatenate([passage_ids, targets.reshape(-1)])
    embedded_part = jnp.take(vocab_table, all_ids, axis=0)
    piece = lax.all_gather(embedded_part, ("mp", "segment"), axis=1, tiled=True)
    passage_part = embedded_part[:pass_rows]
    target_part = embedded_part[pass_rows:]
    rows_f32 = piece.astype(jnp.float32)
    scale = lax.rsqrt(jnp.sum(rows_f32 * rows_f32, axis=1) / D + epsilon)
    pass_normed = (rows_f32[:pass_rows] * norm_gains[0]).astype(jnp.bfloat16)
    targ_normed = (rows_f32[pass_rows:] * norm_gains[1]).astype(jnp.bfloat16)

    accum = project(pass_normed, enc_pieces, shard_rows)
    projected = (accum * scale[:pass_rows, None, None]).astype(jnp.bfloat16)
    shaped = projected.reshape(per_question, length, 3, head_block)
    context = attend(shaped[:, :, 0], shaped[:, :, 1], shaped[:, :, 2], head_count)
    enc_partial = lax.dot_general(
        context,
        in_order(enc_out_pieces, shard_rows),
        (((1,), (1,)), ((), ())),
        preferred_element_type=jnp.float32,
    )
    encoded = (
        passage_part.astype(jnp.float32)
        + lax.psum_scatter(
            enc_partial.astype(jnp.bfloat16), ("mp", "segment"), scatter_dimension=1, tiled=True
        ).astype(jnp.float32)
    ).astype(jnp.bfloat16)

    enc_f32 = lax.all_gather(encoded, ("mp", "segment"), axis=1, tiled=True).astype(jnp.float32)
    enc_scale = lax.rsqrt(jnp.sum(enc_f32 * enc_f32, axis=1) / D + epsilon)
    enc_normed = (enc_f32 * norm_gains[2]).astype(jnp.bfloat16)
    query_pieces = [(o, f, b[0:1]) for o, f, b in dec_pieces]
    cross_pieces = [(o, f, b[1:3]) for o, f, b in dec_pieces]
    targ_accum = project(targ_normed, query_pieces, shard_rows)[:, 0]
    queries = (targ_accum * scale[pass_rows:, None]).astype(jnp.bfloat16)[None]
    cross_accum = project(enc_normed, cross_pieces, shard_rows)
    key_values = (cross_accum * enc_scale[:, None, None]).astype(jnp.bfloat16)
    dec_context = attend(queries, key_values[None, :, 0], key_values[None, :, 1], head_count)
    dec_partial = lax.dot_general(
        dec_context,
        in_order(dec_out_pieces, shard_rows),
        (((1,), (1,)), ((), ())),
        preferred_element_type=jnp.float32,
    )
    decoded = (
        target_part.astype(jnp.float32)
        + lax.psum_scatter(
            dec_partial.astype(jnp.bfloat16), ("mp", "segment"), scatter_dimension=1, tiled=True
        ).astype(jnp.float32)
    ).astype(jnp.bfloat16)
    return (encoded, decoded)


def solution(mesh):
    placed = (
        P("shard", None),
        P(),
        P(),
        P("shard", None),
        P(None, ("mp", "segment")),
        P(),
        P("segment", None, "shard", "mp"),
    )
    return jax.shard_map(
        body,
        mesh=mesh,
        in_specs=placed,
        out_specs=(P("shard", ("mp", "segment")), P("shard", ("mp", "segment"))),
        check_vma=False,
    )
```

```python
import jax
import jax.numpy as jnp
from jax import lax
from jax.sharding import PartitionSpec as P

D = 4096
DH = 64


epsilon = 1e-06


def attend(query_rows, key_rows, value_rows, head_count):
    batch_size = query_rows.shape[0]
    head_size = query_rows.shape[2] // head_count
    query_heads = query_rows.reshape(batch_size, query_rows.shape[1], head_count, head_size)
    key_heads = key_rows.reshape(batch_size, key_rows.shape[1], head_count, head_size)
    value_heads = value_rows.reshape(batch_size, value_rows.shape[1], head_count, head_size)
    scores = jnp.einsum(
        "brhd,bshd->bhrs", query_heads, key_heads, preferred_element_type=jnp.float32
    ) * head_size ** (-0.5)
    shifted = jnp.exp(scores - jnp.max(scores, axis=-1, keepdims=True))
    attention = (shifted / jnp.sum(shifted, axis=-1, keepdims=True)).astype(jnp.bfloat16)
    mixture = jnp.einsum(
        "bhrs,bshd->brhd", attention, value_heads, preferred_element_type=jnp.float32
    )
    return mixture.astype(jnp.bfloat16).reshape(
        batch_size * query_rows.shape[1], head_count * head_size
    )


def after(value, *others):
    return lax.optimization_barrier((value,) + others)[0]


def swap_segments(weights, first, count):
    me = lax.axis_index("segment")
    rows, half = weights.shape[2], weights.shape[3] // 2
    size = (1, count, rows, half)
    kept = lax.dynamic_slice(weights, (0, first, 0, me * half), size)[0]
    sent = lax.dynamic_slice(weights, (0, first, 0, (1 - me) * half), size)[0]
    other = lax.ppermute(sent, "segment", [(0, 1), (1, 0)])
    encoder = jnp.where(me == 0, kept, other)

    def decoder(*others):
        late_kept, late_other = lax.optimization_barrier((kept, other) + others)[:2]
        return jnp.where(me == 0, late_other, late_kept)

    return encoder, decoder


X_PAIRS = [(i, i ^ 1) for i in range(4)]
Y_PAIRS = [(i, i ^ 2) for i in range(4)]


def near(block):
    count = lax.axis_size("shard")
    me = lax.axis_index("shard")
    rows = block.shape[1]
    if count != 4:
        whole = lax.all_gather(block, "shard", axis=1, tiled=True)
        return [(i, 0, whole[:, i * rows : (i + 1) * rows]) for i in range(count)]
    return [
        (me, 0, block),
        (me ^ 1, 0, lax.ppermute(block, "shard", X_PAIRS)),
        (me ^ 2, 0, lax.ppermute(block, "shard", Y_PAIRS)),
    ]


def far(pieces):
    if lax.axis_size("shard") != 4:
        return []
    me = lax.axis_index("shard")
    rows = pieces[0][2].shape[1]
    top = lax.ppermute(pieces[2][2][:, : rows // 2], "shard", X_PAIRS)
    bottom = lax.ppermute(pieces[1][2][:, rows // 2 :], "shard", Y_PAIRS)
    return [(me ^ 3, 0, top), (me ^ 3, rows // 2, bottom)]


def blocks(pieces):
    return [piece[2] for piece in pieces]


def pick(pieces, first, stop):
    return [(owner, row, block[first:stop]) for owner, row, block in pieces]


def project(rows_in, pieces, shard_rows, total=None):
    for owner, first, block in pieces:
        depth = block.shape[1]
        part = lax.dynamic_slice_in_dim(rows_in, owner * shard_rows + first, depth, axis=1)
        term = jnp.einsum("rn,knh->rkh", part, block, preferred_element_type=jnp.float32)
        total = term if total is None else total + term
    return total


def in_order(pieces, shard_rows):
    columns = pieces[0][2].shape[2]
    whole = jnp.zeros((D, columns), jnp.bfloat16)
    for owner, first, block in pieces:
        whole = lax.dynamic_update_slice_in_dim(
            whole, block[0], owner * shard_rows + first, axis=0
        )
    return whole


def body(store_tokens, retrieved, owner_shard, targets, vocab_table, norm_gains, layer_weights):
    shard_count = lax.axis_size("shard")
    my_shard = lax.axis_index("shard")
    enc_qkv, dec_qkv = swap_segments(layer_weights, 0, 3)
    per_question = retrieved.shape[1]
    length = store_tokens.shape[1]
    slot_cap = max(2, (per_question + shard_count - 1) // shard_count)
    owners = owner_shard.reshape(retrieved.shape)
    positions = jnp.arange(per_question)
    before = positions[None, :] < positions[:, None]
    matches = owners[:, :, None] == owners[:, None, :]
    slot_rank = jnp.sum(jnp.where(matches & before[None], 1, 0), axis=2).astype(jnp.int32)
    slot_numbers = jnp.arange(slot_cap)
    chosen = (owners[:, None, :] == my_shard) & (
        slot_rank[:, None, :] == slot_numbers[None, :, None]
    )
    local_rows = jnp.sum(jnp.where(chosen, retrieved[:, None, :], 0), axis=2)
    send_ids = jnp.take(store_tokens, local_rows.reshape(-1), axis=0).reshape(
        shard_count, slot_cap, length
    )
    send_ids = after(send_ids, enc_qkv)
    arrived = lax.all_to_all(send_ids, "shard", split_axis=0, concat_axis=0, tiled=True)
    mine_owner = lax.dynamic_index_in_dim(owners, my_shard, 0, keepdims=False)
    mine_rank = lax.dynamic_index_in_dim(slot_rank, my_shard, 0, keepdims=False)
    arrived_rows = arrived.reshape(shard_count * slot_cap, length)
    passage_ids = jnp.take(arrived_rows, mine_owner * slot_cap + mine_rank, axis=0).reshape(-1)
    enc_out, dec_out = swap_segments(layer_weights, 3, 1)
    shard_rows = layer_weights.shape[2]
    head_block = enc_qkv.shape[2]
    head_count = head_block // DH
    pass_rows = passage_ids.shape[0]
    all_ids = jnp.concatenate([passage_ids, targets.reshape(-1)])
    embedded_part = jnp.take(vocab_table, all_ids, axis=0)
    piece = lax.all_gather(embedded_part, ("mp", "segment"), axis=1, tiled=True)
    passage_part = embedded_part[:pass_rows]
    target_part = embedded_part[pass_rows:]
    rows_f32 = piece.astype(jnp.float32)
    scale = lax.rsqrt(jnp.sum(rows_f32 * rows_f32, axis=1) / D + epsilon)
    pass_normed = (rows_f32[:pass_rows] * norm_gains[0]).astype(jnp.bfloat16)
    targ_normed = (rows_f32[pass_rows:] * norm_gains[1]).astype(jnp.bfloat16)

    enc_near = near(enc_qkv)
    accum = project(pass_normed, enc_near, shard_rows)
    enc_far = far(enc_near)
    out_near = near(after(enc_out, accum))
    accum = project(pass_normed, enc_far, shard_rows, accum)
    cross_near = near(dec_qkv(*blocks(out_near))[1:3])
    out_far = far(out_near)
    projected = (accum * scale[:pass_rows, None, None]).astype(jnp.bfloat16)
    shaped = projected.reshape(per_question, length, 3, head_block)
    context = attend(shaped[:, :, 0], shaped[:, :, 1], shaped[:, :, 2], head_count)
    enc_partial = lax.dot_general(
        context,
        in_order(out_near + out_far, shard_rows),
        (((1,), (1,)), ((), ())),
        preferred_element_type=jnp.float32,
    ).astype(jnp.bfloat16)
    enc_sum = lax.psum_scatter(
        enc_partial, ("mp", "segment"), scatter_dimension=1, tiled=True
    ).astype(jnp.float32)
    enc_sum = after(enc_sum, *blocks(cross_near))
    encoded = (passage_part.astype(jnp.float32) + enc_sum).astype(jnp.bfloat16)

    whole_encoded = lax.all_gather(encoded, ("mp", "segment"), axis=1, tiled=True)
    cross_far = far(cross_near)
    late = jnp.concatenate(
        [dec_qkv(*blocks(cross_near))[0:1], dec_out(*blocks(cross_near))], axis=0
    )
    late_near = near(late)
    whole_encoded = after(whole_encoded, *blocks(cross_far), *blocks(late_near))
    late_far = far(late_near)
    enc_f32 = whole_encoded.astype(jnp.float32)
    enc_scale = lax.rsqrt(jnp.sum(enc_f32 * enc_f32, axis=1) / D + epsilon)
    enc_normed = (enc_f32 * norm_gains[2]).astype(jnp.bfloat16)
    cross_accum = project(enc_normed, cross_near + cross_far, shard_rows)
    key_values = (cross_accum * enc_scale[:, None, None]).astype(jnp.bfloat16)
    targ_accum = project(targ_normed, pick(late_near + late_far, 0, 1), shard_rows)[:, 0]
    queries = (targ_accum * scale[pass_rows:, None]).astype(jnp.bfloat16)[None]
    dec_context = attend(queries, key_values[None, :, 0], key_values[None, :, 1], head_count)
    dec_partial = lax.dot_general(
        dec_context,
        in_order(pick(late_near + late_far, 1, 2), shard_rows),
        (((1,), (1,)), ((), ())),
        preferred_element_type=jnp.float32,
    ).astype(jnp.bfloat16)
    terms = lax.all_to_all(
        dec_partial, ("mp", "segment"), split_axis=1, concat_axis=0, tiled=True
    )
    terms = terms.reshape(-1, target_part.shape[0], target_part.shape[1]).astype(jnp.float32)
    decoded = (target_part.astype(jnp.float32) + jnp.sum(terms, axis=0)).astype(jnp.bfloat16)
    return (encoded, decoded)


def solution(mesh):
    placed = (
        P("shard", None),
        P(),
        P(),
        P("shard", None),
        P(None, ("mp", "segment")),
        P(),
        P("segment", None, "shard", "mp"),
    )
    return jax.shard_map(
        body,
        mesh=mesh,
        in_specs=placed,
        out_specs=(P("shard", ("mp", "segment")), P("shard", ("mp", "segment"))),
        check_vma=False,
    )
```

```python
import jax
import jax.numpy as jnp
from jax import lax
from jax.sharding import PartitionSpec as P

D = 4096
DH = 64


epsilon = 1e-06


def attend(query_rows, key_rows, value_rows, head_count):
    batch_size = query_rows.shape[0]
    head_size = query_rows.shape[2] // head_count
    query_heads = query_rows.reshape(batch_size, query_rows.shape[1], head_count, head_size)
    key_heads = key_rows.reshape(batch_size, key_rows.shape[1], head_count, head_size)
    value_heads = value_rows.reshape(batch_size, value_rows.shape[1], head_count, head_size)
    scores = jnp.einsum(
        "brhd,bshd->bhrs", query_heads, key_heads, preferred_element_type=jnp.float32
    ) * head_size ** (-0.5)
    shifted = jnp.exp(scores - jnp.max(scores, axis=-1, keepdims=True))
    attention = (shifted / jnp.sum(shifted, axis=-1, keepdims=True)).astype(jnp.bfloat16)
    mixture = jnp.einsum(
        "bhrs,bshd->brhd", attention, value_heads, preferred_element_type=jnp.float32
    )
    return mixture.astype(jnp.bfloat16).reshape(
        batch_size * query_rows.shape[1], head_count * head_size
    )


def after(value, *others):
    return lax.optimization_barrier((value,) + others)[0]


def swap_segments(weights, first, count):
    me = lax.axis_index("segment")
    rows, half = weights.shape[2], weights.shape[3] // 2
    size = (1, count, rows, half)
    kept = lax.dynamic_slice(weights, (0, first, 0, me * half), size)[0]
    sent = lax.dynamic_slice(weights, (0, first, 0, (1 - me) * half), size)[0]
    other = lax.ppermute(sent, "segment", [(0, 1), (1, 0)])
    encoder = jnp.where(me == 0, kept, other)

    def decoder(*others):
        late_kept, late_other = lax.optimization_barrier((kept, other) + others)[:2]
        return jnp.where(me == 0, late_other, late_kept)

    return encoder, decoder


X_PAIRS = [(i, i ^ 1) for i in range(4)]
Y_PAIRS = [(i, i ^ 2) for i in range(4)]


def near(block):
    count = lax.axis_size("shard")
    me = lax.axis_index("shard")
    rows = block.shape[1]
    if count != 4:
        whole = lax.all_gather(block, "shard", axis=1, tiled=True)
        return [(i, 0, whole[:, i * rows : (i + 1) * rows]) for i in range(count)]
    return [
        (me, 0, block),
        (me ^ 1, 0, lax.ppermute(block, "shard", X_PAIRS)),
        (me ^ 2, 0, lax.ppermute(block, "shard", Y_PAIRS)),
    ]


def far(pieces):
    if lax.axis_size("shard") != 4:
        return []
    me = lax.axis_index("shard")
    rows = pieces[0][2].shape[1]
    top = lax.ppermute(pieces[2][2][:, : rows // 2], "shard", X_PAIRS)
    bottom = lax.ppermute(pieces[1][2][:, rows // 2 :], "shard", Y_PAIRS)
    return [(me ^ 3, 0, top), (me ^ 3, rows // 2, bottom)]


def blocks(pieces):
    return [piece[2] for piece in pieces]


def project(rows_in, pieces, shard_rows, total=None):
    for owner, first, block in pieces:
        depth = block.shape[1]
        part = lax.dynamic_slice_in_dim(rows_in, owner * shard_rows + first, depth, axis=1)
        term = jnp.einsum("rn,knh->rkh", part, block, preferred_element_type=jnp.float32)
        total = term if total is None else total + term
    return total


def in_order(pieces, shard_rows):
    columns = pieces[0][2].shape[2]
    whole = jnp.zeros((D, columns), jnp.bfloat16)
    for owner, first, block in pieces:
        whole = lax.dynamic_update_slice_in_dim(
            whole, block[0], owner * shard_rows + first, axis=0
        )
    return whole


def body(store_tokens, retrieved, owner_shard, targets, vocab_table, norm_gains, layer_weights):
    shard_count = lax.axis_size("shard")
    my_shard = lax.axis_index("shard")
    enc_qkv, dec_qkv = swap_segments(layer_weights, 0, 3)
    per_question = retrieved.shape[1]
    length = store_tokens.shape[1]
    slot_cap = max(2, (per_question + shard_count - 1) // shard_count)
    owners = owner_shard.reshape(retrieved.shape)
    positions = jnp.arange(per_question)
    before = positions[None, :] < positions[:, None]
    matches = owners[:, :, None] == owners[:, None, :]
    slot_rank = jnp.sum(jnp.where(matches & before[None], 1, 0), axis=2).astype(jnp.int32)
    slot_numbers = jnp.arange(slot_cap)
    chosen = (owners[:, None, :] == my_shard) & (
        slot_rank[:, None, :] == slot_numbers[None, :, None]
    )
    local_rows = jnp.sum(jnp.where(chosen, retrieved[:, None, :], 0), axis=2)
    send_ids = jnp.take(store_tokens, local_rows.reshape(-1), axis=0).reshape(
        shard_count, slot_cap, length
    )
    send_ids = after(send_ids, enc_qkv)
    arrived = lax.all_to_all(send_ids, "shard", split_axis=0, concat_axis=0, tiled=True)
    mine_owner = lax.dynamic_index_in_dim(owners, my_shard, 0, keepdims=False)
    mine_rank = lax.dynamic_index_in_dim(slot_rank, my_shard, 0, keepdims=False)
    arrived_rows = arrived.reshape(shard_count * slot_cap, length)
    passage_ids = jnp.take(arrived_rows, mine_owner * slot_cap + mine_rank, axis=0).reshape(-1)
    enc_out, dec_out = swap_segments(layer_weights, 3, 1)
    shard_rows = layer_weights.shape[2]
    head_block = enc_qkv.shape[2]
    head_count = head_block // DH
    pass_rows = passage_ids.shape[0]
    all_ids = jnp.concatenate([passage_ids, targets.reshape(-1)])
    embedded_part = jnp.take(vocab_table, all_ids, axis=0)
    piece = lax.all_gather(embedded_part, ("mp", "segment"), axis=1, tiled=True)
    passage_part = embedded_part[:pass_rows]
    target_part = embedded_part[pass_rows:]
    rows_f32 = piece.astype(jnp.float32)
    scale = lax.rsqrt(jnp.sum(rows_f32 * rows_f32, axis=1) / D + epsilon)
    pass_normed = (rows_f32[:pass_rows] * norm_gains[0]).astype(jnp.bfloat16)
    targ_normed = (rows_f32[pass_rows:] * norm_gains[1]).astype(jnp.bfloat16)

    enc_near = near(enc_qkv)
    accum = project(pass_normed, enc_near, shard_rows)
    enc_far = far(enc_near)
    out_near = near(after(enc_out, accum))
    accum = project(pass_normed, enc_far, shard_rows, accum)
    cross_near = near(dec_qkv(*blocks(out_near))[1:3])
    out_far = far(out_near)
    projected = (accum * scale[:pass_rows, None, None]).astype(jnp.bfloat16)
    shaped = projected.reshape(per_question, length, 3, head_block)
    values = after(shaped[:, :, 2], *blocks(out_near))
    context = attend(shaped[:, :, 0], shaped[:, :, 1], values, head_count)
    enc_partial = lax.dot_general(
        context,
        in_order(out_near + out_far, shard_rows),
        (((1,), (1,)), ((), ())),
        preferred_element_type=jnp.float32,
    ).astype(jnp.bfloat16)
    enc_sum = lax.psum_scatter(
        enc_partial, ("mp", "segment"), scatter_dimension=1, tiled=True
    ).astype(jnp.float32)
    query_rows = lax.all_to_all(
        after(targ_normed, enc_partial), "shard", split_axis=1, concat_axis=0, tiled=True
    )
    query_terms = jnp.dot(
        query_rows, dec_qkv(enc_partial)[0], preferred_element_type=jnp.float32
    )
    query_terms = lax.all_to_all(query_terms, "shard", split_axis=0, concat_axis=0, tiled=True)
    targ_accum = jnp.sum(query_terms.reshape(shard_count, -1, head_block), axis=0)
    queries = (targ_accum * scale[pass_rows:, None]).astype(jnp.bfloat16)[None]
    enc_sum = after(enc_sum, queries, *blocks(cross_near))
    encoded = (passage_part.astype(jnp.float32) + enc_sum).astype(jnp.bfloat16)

    whole_encoded = lax.all_gather(encoded, ("mp", "segment"), axis=1, tiled=True)
    cross_far = far(cross_near)
    late_near = near(dec_out(*blocks(cross_near)))
    whole_encoded = after(whole_encoded, *blocks(cross_far), *blocks(late_near))
    late_far = far(late_near)
    enc_f32 = whole_encoded.astype(jnp.float32)
    enc_scale = lax.rsqrt(jnp.sum(enc_f32 * enc_f32, axis=1) / D + epsilon)
    enc_normed = (enc_f32 * norm_gains[2]).astype(jnp.bfloat16)
    cross_accum = project(enc_normed, cross_near + cross_far, shard_rows)
    key_values = (cross_accum * enc_scale[:, None, None]).astype(jnp.bfloat16)
    dec_context = attend(queries, key_values[None, :, 0], key_values[None, :, 1], head_count)
    dec_partial = lax.dot_general(
        dec_context,
        in_order(late_near + late_far, shard_rows),
        (((1,), (1,)), ((), ())),
        preferred_element_type=jnp.float32,
    ).astype(jnp.bfloat16)
    terms = lax.all_to_all(
        dec_partial, ("mp", "segment"), split_axis=1, concat_axis=0, tiled=True
    )
    terms = terms.reshape(-1, target_part.shape[0], target_part.shape[1]).astype(jnp.float32)
    decoded = (target_part.astype(jnp.float32) + jnp.sum(terms, axis=0)).astype(jnp.bfloat16)
    return (encoded, decoded)


def solution(mesh):
    placed = (
        P("shard", None),
        P(),
        P(),
        P("shard", None),
        P(None, ("mp", "segment")),
        P(),
        P("segment", None, "shard", "mp"),
    )
    return jax.shard_map(
        body,
        mesh=mesh,
        in_specs=placed,
        out_specs=(P("shard", ("mp", "segment")), P("shard", ("mp", "segment"))),
        check_vma=False,
    )
```

```python
import jax
import jax.numpy as jnp
from jax import lax
from jax.sharding import PartitionSpec as P

D = 4096
DH = 64


epsilon = 1e-06


def attend(query_rows, key_rows, value_rows, head_count):
    batch_size = query_rows.shape[0]
    head_size = query_rows.shape[2] // head_count
    query_heads = query_rows.reshape(batch_size, query_rows.shape[1], head_count, head_size)
    key_heads = key_rows.reshape(batch_size, key_rows.shape[1], head_count, head_size)
    value_heads = value_rows.reshape(batch_size, value_rows.shape[1], head_count, head_size)
    scores = jnp.einsum(
        "brhd,bshd->bhrs", query_heads, key_heads, preferred_element_type=jnp.float32
    ) * head_size ** (-0.5)
    shifted = jnp.exp(scores - jnp.max(scores, axis=-1, keepdims=True))
    attention = (shifted / jnp.sum(shifted, axis=-1, keepdims=True)).astype(jnp.bfloat16)
    mixture = jnp.einsum(
        "bhrs,bshd->brhd", attention, value_heads, preferred_element_type=jnp.float32
    )
    return mixture.astype(jnp.bfloat16).reshape(
        batch_size * query_rows.shape[1], head_count * head_size
    )


def after(value, *others):
    return lax.optimization_barrier((value,) + others)[0]


def swap_segments(weights, first, count):
    me = lax.axis_index("segment")
    rows, half = weights.shape[2], weights.shape[3] // 2
    size = (1, count, rows, half)
    kept = lax.dynamic_slice(weights, (0, first, 0, me * half), size)[0]
    sent = lax.dynamic_slice(weights, (0, first, 0, (1 - me) * half), size)[0]
    other = lax.ppermute(sent, "segment", [(0, 1), (1, 0)])
    encoder = jnp.where(me == 0, kept, other)

    def decoder(*others):
        late_kept, late_other = lax.optimization_barrier((kept, other) + others)[:2]
        return jnp.where(me == 0, late_other, late_kept)

    return encoder, decoder


X_PAIRS = [(i, i ^ 1) for i in range(4)]
Y_PAIRS = [(i, i ^ 2) for i in range(4)]


def near(block):
    count = lax.axis_size("shard")
    me = lax.axis_index("shard")
    rows = block.shape[1]
    if count != 4:
        whole = lax.all_gather(block, "shard", axis=1, tiled=True)
        return [(i, 0, whole[:, i * rows : (i + 1) * rows]) for i in range(count)]
    return [
        (me, 0, block),
        (me ^ 1, 0, lax.ppermute(block, "shard", X_PAIRS)),
        (me ^ 2, 0, lax.ppermute(block, "shard", Y_PAIRS)),
    ]


def far(pieces):
    if lax.axis_size("shard") != 4:
        return []
    me = lax.axis_index("shard")
    rows = pieces[0][2].shape[1]
    top = lax.ppermute(pieces[2][2][:, : rows // 2], "shard", X_PAIRS)
    bottom = lax.ppermute(pieces[1][2][:, rows // 2 :], "shard", Y_PAIRS)
    return [(me ^ 3, 0, top), (me ^ 3, rows // 2, bottom)]


def blocks(pieces):
    return [piece[2] for piece in pieces]


def project(rows_in, pieces, shard_rows, total=None):
    for owner, first, block in pieces:
        depth = block.shape[1]
        part = lax.dynamic_slice_in_dim(rows_in, owner * shard_rows + first, depth, axis=1)
        term = jnp.einsum("rn,knh->rkh", part, block, preferred_element_type=jnp.float32)
        total = term if total is None else total + term
    return total


def in_order(pieces, shard_rows):
    columns = pieces[0][2].shape[2]
    whole = jnp.zeros((D, columns), jnp.bfloat16)
    for owner, first, block in pieces:
        whole = lax.dynamic_update_slice_in_dim(
            whole, block[0], owner * shard_rows + first, axis=0
        )
    return whole


def body(store_tokens, retrieved, owner_shard, targets, vocab_table, norm_gains, layer_weights):
    shard_count = lax.axis_size("shard")
    my_shard = lax.axis_index("shard")
    enc_qkv, dec_qkv = swap_segments(layer_weights, 0, 3)
    per_question = retrieved.shape[1]
    length = store_tokens.shape[1]
    slot_cap = max(2, (per_question + shard_count - 1) // shard_count)
    owners = owner_shard.reshape(retrieved.shape)
    positions = jnp.arange(per_question)
    before = positions[None, :] < positions[:, None]
    matches = owners[:, :, None] == owners[:, None, :]
    slot_rank = jnp.sum(jnp.where(matches & before[None], 1, 0), axis=2).astype(jnp.int32)
    slot_numbers = jnp.arange(slot_cap)
    chosen = (owners[:, None, :] == my_shard) & (
        slot_rank[:, None, :] == slot_numbers[None, :, None]
    )
    local_rows = jnp.sum(jnp.where(chosen, retrieved[:, None, :], 0), axis=2)
    send_ids = jnp.take(store_tokens, local_rows.reshape(-1), axis=0).reshape(
        shard_count, slot_cap, length
    )
    arrived = lax.all_to_all(send_ids, "shard", split_axis=0, concat_axis=0, tiled=True)
    mine_owner = lax.dynamic_index_in_dim(owners, my_shard, 0, keepdims=False)
    mine_rank = lax.dynamic_index_in_dim(slot_rank, my_shard, 0, keepdims=False)
    arrived_rows = arrived.reshape(shard_count * slot_cap, length)
    passage_ids = jnp.take(arrived_rows, mine_owner * slot_cap + mine_rank, axis=0).reshape(-1)
    enc_out, dec_out = swap_segments(layer_weights, 3, 1)
    shard_rows = layer_weights.shape[2]
    head_block = enc_qkv.shape[2]
    head_count = head_block // DH
    pass_rows = passage_ids.shape[0]
    all_ids = after(jnp.concatenate([passage_ids, targets.reshape(-1)]), enc_qkv)
    embedded_part = jnp.take(vocab_table, all_ids, axis=0)
    piece = lax.all_gather(embedded_part, ("mp", "segment"), axis=1, tiled=True)
    passage_part = embedded_part[:pass_rows]
    target_part = embedded_part[pass_rows:]
    rows_f32 = piece.astype(jnp.float32)
    scale = lax.rsqrt(jnp.sum(rows_f32 * rows_f32, axis=1) / D + epsilon)
    pass_normed = (rows_f32[:pass_rows] * norm_gains[0]).astype(jnp.bfloat16)
    targ_normed = (rows_f32[pass_rows:] * norm_gains[1]).astype(jnp.bfloat16)

    enc_near = near(enc_qkv)
    accum = project(pass_normed, enc_near, shard_rows)
    enc_far = far(enc_near)
    out_near = near(after(enc_out, accum))
    accum = project(pass_normed, enc_far, shard_rows, accum)
    cross_near = near(dec_qkv(*blocks(out_near))[1:3])
    out_far = far(out_near)
    projected = (accum * scale[:pass_rows, None, None]).astype(jnp.bfloat16)
    shaped = projected.reshape(per_question, length, 3, head_block)
    values = after(shaped[:, :, 2], *blocks(out_near))
    context = attend(shaped[:, :, 0], shaped[:, :, 1], values, head_count)
    enc_partial = lax.dot_general(
        context,
        in_order(out_near + out_far, shard_rows),
        (((1,), (1,)), ((), ())),
        preferred_element_type=jnp.float32,
    ).astype(jnp.bfloat16)
    enc_sum = lax.psum_scatter(
        enc_partial, ("mp", "segment"), scatter_dimension=1, tiled=True
    ).astype(jnp.float32)
    query_rows = lax.all_to_all(
        after(targ_normed, enc_partial), "shard", split_axis=1, concat_axis=0, tiled=True
    )
    query_terms = jnp.dot(
        query_rows, dec_qkv(enc_partial)[0], preferred_element_type=jnp.float32
    )
    query_terms = lax.all_to_all(query_terms, "shard", split_axis=0, concat_axis=0, tiled=True)
    targ_accum = jnp.sum(query_terms.reshape(shard_count, -1, head_block), axis=0)
    queries = (targ_accum * scale[pass_rows:, None]).astype(jnp.bfloat16)[None]
    enc_sum = after(enc_sum, queries, *blocks(cross_near))
    encoded = (passage_part.astype(jnp.float32) + enc_sum).astype(jnp.bfloat16)

    whole_encoded = lax.all_gather(encoded, ("mp", "segment"), axis=1, tiled=True)
    cross_far = far(cross_near)
    late_near = near(dec_out(*blocks(cross_far)))
    whole_encoded = after(whole_encoded, *blocks(cross_far), *blocks(late_near))
    enc_f32 = whole_encoded.astype(jnp.float32)
    enc_scale = lax.rsqrt(jnp.sum(enc_f32 * enc_f32, axis=1) / D + epsilon)
    late_far = far([(o, f, after(b, enc_scale)) for o, f, b in late_near])
    enc_normed = (enc_f32 * norm_gains[2]).astype(jnp.bfloat16)
    cross_accum = project(enc_normed, cross_near + cross_far, shard_rows)
    key_values = (cross_accum * enc_scale[:, None, None]).astype(jnp.bfloat16)
    dec_context = attend(queries, key_values[None, :, 0], key_values[None, :, 1], head_count)
    dec_partial = lax.dot_general(
        dec_context,
        in_order(late_near + late_far, shard_rows),
        (((1,), (1,)), ((), ())),
        preferred_element_type=jnp.float32,
    ).astype(jnp.bfloat16)
    terms = lax.all_to_all(
        dec_partial, ("mp", "segment"), split_axis=1, concat_axis=0, tiled=True
    )
    terms = terms.reshape(-1, target_part.shape[0], target_part.shape[1]).astype(jnp.float32)
    decoded = (target_part.astype(jnp.float32) + jnp.sum(terms, axis=0)).astype(jnp.bfloat16)
    return (encoded, decoded)


def solution(mesh):
    placed = (
        P("shard", None),
        P(),
        P(),
        P("shard", None),
        P(None, ("mp", "segment")),
        P(),
        P("segment", None, "shard", "mp"),
    )
    return jax.shard_map(
        body,
        mesh=mesh,
        in_specs=placed,
        out_specs=(P("shard", ("mp", "segment")), P("shard", ("mp", "segment"))),
        check_vma=False,
    )
```

```python
import jax
import jax.numpy as jnp
from jax import lax
from jax.sharding import PartitionSpec as P

D = 4096
DH = 64


epsilon = 1e-06


def attend(query_rows, key_rows, value_rows, head_count):
    batch_size = query_rows.shape[0]
    head_size = query_rows.shape[2] // head_count
    query_heads = query_rows.reshape(batch_size, query_rows.shape[1], head_count, head_size)
    key_heads = key_rows.reshape(batch_size, key_rows.shape[1], head_count, head_size)
    value_heads = value_rows.reshape(batch_size, value_rows.shape[1], head_count, head_size)
    scores = jnp.einsum(
        "brhd,bshd->bhrs", query_heads, key_heads, preferred_element_type=jnp.float32
    ) * head_size ** (-0.5)
    shifted = jnp.exp(scores - jnp.max(scores, axis=-1, keepdims=True))
    attention = (shifted / jnp.sum(shifted, axis=-1, keepdims=True)).astype(jnp.bfloat16)
    mixture = jnp.einsum(
        "bhrs,bshd->brhd", attention, value_heads, preferred_element_type=jnp.float32
    )
    return mixture.astype(jnp.bfloat16).reshape(
        batch_size * query_rows.shape[1], head_count * head_size
    )


def after(value, *others):
    return lax.optimization_barrier((value,) + others)[0]


def swap_segments(weights, first, count):
    me = lax.axis_index("segment")
    rows, half = weights.shape[2], weights.shape[3] // 2
    size = (1, count, rows, half)
    kept = lax.dynamic_slice(weights, (0, first, 0, me * half), size)[0]
    sent = lax.dynamic_slice(weights, (0, first, 0, (1 - me) * half), size)[0]
    other = lax.ppermute(sent, "segment", [(0, 1), (1, 0)])
    encoder = jnp.where(me == 0, kept, other)

    def decoder(*others):
        late_kept, late_other = lax.optimization_barrier((kept, other) + others)[:2]
        return jnp.where(me == 0, late_other, late_kept)

    return encoder, decoder


X_PAIRS = [(i, i ^ 1) for i in range(4)]
Y_PAIRS = [(i, i ^ 2) for i in range(4)]


def near(block):
    count = lax.axis_size("shard")
    me = lax.axis_index("shard")
    rows = block.shape[1]
    if count != 4:
        whole = lax.all_gather(block, "shard", axis=1, tiled=True)
        return [(i, 0, whole[:, i * rows : (i + 1) * rows]) for i in range(count)]
    return [
        (me, 0, block),
        (me ^ 1, 0, lax.ppermute(block, "shard", X_PAIRS)),
        (me ^ 2, 0, lax.ppermute(block, "shard", Y_PAIRS)),
    ]


def far(pieces):
    if lax.axis_size("shard") != 4:
        return []
    me = lax.axis_index("shard")
    rows = pieces[0][2].shape[1]
    top = lax.ppermute(pieces[2][2][:, : rows // 2], "shard", X_PAIRS)
    bottom = lax.ppermute(pieces[1][2][:, rows // 2 :], "shard", Y_PAIRS)
    return [(me ^ 3, 0, top), (me ^ 3, rows // 2, bottom)]


def blocks(pieces):
    return [piece[2] for piece in pieces]


def project(rows_in, pieces, shard_rows, total=None):
    for owner, first, block in pieces:
        depth = block.shape[1]
        part = lax.dynamic_slice_in_dim(rows_in, owner * shard_rows + first, depth, axis=1)
        term = jnp.einsum("rn,knh->rkh", part, block, preferred_element_type=jnp.float32)
        total = term if total is None else total + term
    return total


def in_order(pieces, shard_rows):
    columns = pieces[0][2].shape[2]
    whole = jnp.zeros((D, columns), jnp.bfloat16)
    for owner, first, block in pieces:
        whole = lax.dynamic_update_slice_in_dim(
            whole, block[0], owner * shard_rows + first, axis=0
        )
    return whole


def body(store_tokens, retrieved, owner_shard, targets, vocab_table, norm_gains, layer_weights):
    shard_count = lax.axis_size("shard")
    my_shard = lax.axis_index("shard")
    enc_qkv, dec_qkv = swap_segments(layer_weights, 0, 3)
    per_question = retrieved.shape[1]
    length = store_tokens.shape[1]
    slot_cap = max(2, (per_question + shard_count - 1) // shard_count)
    owners = owner_shard.reshape(retrieved.shape)
    positions = jnp.arange(per_question)
    before = positions[None, :] < positions[:, None]
    matches = owners[:, :, None] == owners[:, None, :]
    slot_rank = jnp.sum(jnp.where(matches & before[None], 1, 0), axis=2).astype(jnp.int32)
    slot_numbers = jnp.arange(slot_cap)
    chosen = (owners[:, None, :] == my_shard) & (
        slot_rank[:, None, :] == slot_numbers[None, :, None]
    )
    local_rows = jnp.sum(jnp.where(chosen, retrieved[:, None, :], 0), axis=2)
    send_ids = jnp.take(store_tokens, local_rows.reshape(-1), axis=0).reshape(
        shard_count, slot_cap, length
    )
    arrived = lax.all_to_all(send_ids, "shard", split_axis=0, concat_axis=0, tiled=True)
    mine_owner = lax.dynamic_index_in_dim(owners, my_shard, 0, keepdims=False)
    mine_rank = lax.dynamic_index_in_dim(slot_rank, my_shard, 0, keepdims=False)
    arrived_rows = arrived.reshape(shard_count * slot_cap, length)
    passage_ids = jnp.take(arrived_rows, mine_owner * slot_cap + mine_rank, axis=0).reshape(-1)
    enc_out, dec_out = swap_segments(layer_weights, 3, 1)
    shard_rows = layer_weights.shape[2]
    head_block = enc_qkv.shape[2]
    head_count = head_block // DH
    pass_rows = passage_ids.shape[0]
    all_ids = after(jnp.concatenate([passage_ids, targets.reshape(-1)]), enc_qkv)
    embedded_part = jnp.take(vocab_table, all_ids, axis=0)
    piece = lax.all_gather(embedded_part, ("mp", "segment"), axis=1, tiled=True)
    passage_part = embedded_part[:pass_rows]
    target_part = embedded_part[pass_rows:]
    rows_f32 = piece.astype(jnp.float32)
    scale = lax.rsqrt(jnp.sum(rows_f32 * rows_f32, axis=1) / D + epsilon)
    pass_normed = (rows_f32[:pass_rows] * norm_gains[0]).astype(jnp.bfloat16)
    targ_normed = (rows_f32[pass_rows:] * norm_gains[1]).astype(jnp.bfloat16)

    enc_near = near(enc_qkv)
    accum = project(pass_normed, enc_near, shard_rows)
    enc_far = far(enc_near)
    out_near = near(after(enc_out, accum))
    accum = project(pass_normed, enc_far, shard_rows, accum)
    cross_near = near(dec_qkv(*blocks(out_near))[1:3])
    out_far = far(out_near)
    projected = (accum * scale[:pass_rows, None, None]).astype(jnp.bfloat16)
    shaped = projected.reshape(per_question, length, 3, head_block)
    values = after(shaped[:, :, 2], *blocks(out_near))
    context = attend(shaped[:, :, 0], shaped[:, :, 1], values, head_count)
    enc_partial = lax.dot_general(
        context,
        in_order(out_near + out_far, shard_rows),
        (((1,), (1,)), ((), ())),
        preferred_element_type=jnp.float32,
    ).astype(jnp.bfloat16)
    enc_sum = lax.psum_scatter(
        enc_partial, ("mp", "segment"), scatter_dimension=1, tiled=True
    ).astype(jnp.float32)
    query_rows = lax.all_to_all(
        after(targ_normed, enc_partial), "shard", split_axis=1, concat_axis=0, tiled=True
    )
    query_terms = jnp.dot(
        query_rows, dec_qkv(enc_partial)[0], preferred_element_type=jnp.float32
    )
    query_terms = lax.all_to_all(query_terms, "shard", split_axis=0, concat_axis=0, tiled=True)
    targ_accum = jnp.sum(query_terms.reshape(shard_count, -1, head_block), axis=0)
    queries = (targ_accum * scale[pass_rows:, None]).astype(jnp.bfloat16)[None]
    enc_sum = after(enc_sum, queries, *blocks(cross_near))
    encoded = (passage_part.astype(jnp.float32) + enc_sum).astype(jnp.bfloat16)

    whole_encoded = lax.all_gather(encoded, ("mp", "segment"), axis=1, tiled=True)
    cross_far = far(cross_near)
    late_near = near(dec_out(*blocks(cross_far), queries))
    whole_encoded = after(whole_encoded, *blocks(cross_far))
    enc_f32 = whole_encoded.astype(jnp.float32)
    enc_scale = lax.rsqrt(jnp.sum(enc_f32 * enc_f32, axis=1) / D + epsilon)
    enc_normed = (enc_f32 * norm_gains[2]).astype(jnp.bfloat16)
    cross_accum = project(enc_normed, cross_near + cross_far, shard_rows)
    late_far = far([(o, f, after(b, cross_accum)) for o, f, b in late_near])
    key_values = (cross_accum * enc_scale[:, None, None]).astype(jnp.bfloat16)
    dec_context = attend(queries, key_values[None, :, 0], key_values[None, :, 1], head_count)
    dec_partial = lax.dot_general(
        dec_context,
        in_order(late_near + late_far, shard_rows),
        (((1,), (1,)), ((), ())),
        preferred_element_type=jnp.float32,
    ).astype(jnp.bfloat16)
    terms = lax.all_to_all(
        dec_partial, ("mp", "segment"), split_axis=1, concat_axis=0, tiled=True
    )
    terms = terms.reshape(-1, target_part.shape[0], target_part.shape[1]).astype(jnp.float32)
    decoded = (target_part.astype(jnp.float32) + jnp.sum(terms, axis=0)).astype(jnp.bfloat16)
    return (encoded, decoded)


def solution(mesh):
    placed = (
        P("shard", None),
        P(),
        P(),
        P("shard", None),
        P(None, ("mp", "segment")),
        P(),
        P("segment", None, "shard", "mp"),
    )
    return jax.shard_map(
        body,
        mesh=mesh,
        in_specs=placed,
        out_specs=(P("shard", ("mp", "segment")), P("shard", ("mp", "segment"))),
        check_vma=False,
    )
```

```python
import jax
import jax.numpy as jnp
from jax import lax
from jax.sharding import PartitionSpec as P

D = 4096
DH = 64


epsilon = 1e-06


def attend(query_rows, key_rows, value_rows, head_count):
    batch_size = query_rows.shape[0]
    head_size = query_rows.shape[2] // head_count
    query_heads = query_rows.reshape(batch_size, query_rows.shape[1], head_count, head_size)
    key_heads = key_rows.reshape(batch_size, key_rows.shape[1], head_count, head_size)
    value_heads = value_rows.reshape(batch_size, value_rows.shape[1], head_count, head_size)
    scores = jnp.einsum(
        "brhd,bshd->bhrs", query_heads, key_heads, preferred_element_type=jnp.float32
    ) * head_size ** (-0.5)
    shifted = jnp.exp(scores - jnp.max(scores, axis=-1, keepdims=True))
    attention = (shifted / jnp.sum(shifted, axis=-1, keepdims=True)).astype(jnp.bfloat16)
    mixture = jnp.einsum(
        "bhrs,bshd->brhd", attention, value_heads, preferred_element_type=jnp.float32
    )
    return mixture.astype(jnp.bfloat16).reshape(
        batch_size * query_rows.shape[1], head_count * head_size
    )


def after(value, *others):
    return lax.optimization_barrier((value,) + others)[0]


def swap_segments(weights, first, count):
    me = lax.axis_index("segment")
    rows, half = weights.shape[2], weights.shape[3] // 2
    size = (1, count, rows, half)
    kept = lax.dynamic_slice(weights, (0, first, 0, me * half), size)[0]
    sent = lax.dynamic_slice(weights, (0, first, 0, (1 - me) * half), size)[0]
    other = lax.ppermute(sent, "segment", [(0, 1), (1, 0)])
    encoder = jnp.where(me == 0, kept, other)

    def decoder(*others):
        late_kept, late_other = lax.optimization_barrier((kept, other) + others)[:2]
        return jnp.where(me == 0, late_other, late_kept)

    return encoder, decoder


X_PAIRS = [(i, i ^ 1) for i in range(4)]
Y_PAIRS = [(i, i ^ 2) for i in range(4)]


def near(block):
    count = lax.axis_size("shard")
    me = lax.axis_index("shard")
    rows = block.shape[1]
    if count != 4:
        whole = lax.all_gather(block, "shard", axis=1, tiled=True)
        return [(i, 0, whole[:, i * rows : (i + 1) * rows]) for i in range(count)]
    return [
        (me, 0, block),
        (me ^ 1, 0, lax.ppermute(block, "shard", X_PAIRS)),
        (me ^ 2, 0, lax.ppermute(block, "shard", Y_PAIRS)),
    ]


def far(pieces):
    if lax.axis_size("shard") != 4:
        return []
    me = lax.axis_index("shard")
    rows = pieces[0][2].shape[1]
    top = lax.ppermute(pieces[2][2][:, : rows // 2], "shard", X_PAIRS)
    bottom = lax.ppermute(pieces[1][2][:, rows // 2 :], "shard", Y_PAIRS)
    return [(me ^ 3, 0, top), (me ^ 3, rows // 2, bottom)]


def blocks(pieces):
    return [piece[2] for piece in pieces]


def project(rows_in, pieces, shard_rows, total=None):
    for owner, first, block in pieces:
        depth = block.shape[1]
        part = lax.dynamic_slice_in_dim(rows_in, owner * shard_rows + first, depth, axis=1)
        term = jnp.einsum("rn,knh->rkh", part, block, preferred_element_type=jnp.float32)
        total = term if total is None else total + term
    return total


def in_order(pieces, shard_rows):
    columns = pieces[0][2].shape[2]
    whole = jnp.zeros((D, columns), jnp.bfloat16)
    for owner, first, block in pieces:
        whole = lax.dynamic_update_slice_in_dim(
            whole, block[0], owner * shard_rows + first, axis=0
        )
    return whole


def body(store_tokens, retrieved, owner_shard, targets, vocab_table, norm_gains, layer_weights):
    shard_count = lax.axis_size("shard")
    my_shard = lax.axis_index("shard")
    enc_qkv, dec_qkv = swap_segments(layer_weights, 0, 3)
    per_question = retrieved.shape[1]
    length = store_tokens.shape[1]
    slot_cap = max(2, (per_question + shard_count - 1) // shard_count)
    owners = owner_shard.reshape(retrieved.shape)
    positions = jnp.arange(per_question)
    before = positions[None, :] < positions[:, None]
    matches = owners[:, :, None] == owners[:, None, :]
    slot_rank = jnp.sum(jnp.where(matches & before[None], 1, 0), axis=2).astype(jnp.int32)
    slot_numbers = jnp.arange(slot_cap)
    chosen = (owners[:, None, :] == my_shard) & (
        slot_rank[:, None, :] == slot_numbers[None, :, None]
    )
    local_rows = jnp.sum(jnp.where(chosen, retrieved[:, None, :], 0), axis=2)
    send_ids = jnp.take(store_tokens, local_rows.reshape(-1), axis=0).reshape(
        shard_count, slot_cap, length
    )
    arrived = lax.all_to_all(send_ids, "shard", split_axis=0, concat_axis=0, tiled=True)
    mine_owner = lax.dynamic_index_in_dim(owners, my_shard, 0, keepdims=False)
    mine_rank = lax.dynamic_index_in_dim(slot_rank, my_shard, 0, keepdims=False)
    arrived_rows = arrived.reshape(shard_count * slot_cap, length)
    passage_ids = jnp.take(arrived_rows, mine_owner * slot_cap + mine_rank, axis=0).reshape(-1)
    enc_out, dec_out = swap_segments(layer_weights, 3, 1)
    shard_rows = layer_weights.shape[2]
    head_block = enc_qkv.shape[2]
    head_count = head_block // DH
    pass_rows = passage_ids.shape[0]
    all_ids = after(jnp.concatenate([passage_ids, targets.reshape(-1)]), enc_qkv)
    embedded_part = jnp.take(vocab_table, all_ids, axis=0)
    piece = lax.all_gather(embedded_part, ("mp", "segment"), axis=1, tiled=True)
    passage_part = embedded_part[:pass_rows]
    target_part = embedded_part[pass_rows:]
    rows_f32 = piece.astype(jnp.float32)
    scale = lax.rsqrt(jnp.sum(rows_f32 * rows_f32, axis=1) / D + epsilon)
    pass_normed = (rows_f32[:pass_rows] * norm_gains[0]).astype(jnp.bfloat16)
    targ_normed = (rows_f32[pass_rows:] * norm_gains[1]).astype(jnp.bfloat16)

    enc_near = near(enc_qkv)
    accum = project(pass_normed, enc_near, shard_rows)
    enc_far = far(enc_near)
    out_near = near(after(enc_out, accum))
    accum = project(pass_normed, enc_far, shard_rows, accum)
    cross_near = near(dec_qkv(*blocks(out_near))[1:3])
    out_far = far(out_near)
    projected = (accum * scale[:pass_rows, None, None]).astype(jnp.bfloat16)
    shaped = projected.reshape(per_question, length, 3, head_block)
    context = attend(shaped[:, :, 0], shaped[:, :, 1], shaped[:, :, 2], head_count)
    enc_partial = lax.dot_general(
        context,
        in_order(out_near + out_far, shard_rows),
        (((1,), (1,)), ((), ())),
        preferred_element_type=jnp.float32,
    ).astype(jnp.bfloat16)
    enc_sum = lax.psum_scatter(
        enc_partial, ("mp", "segment"), scatter_dimension=1, tiled=True
    ).astype(jnp.float32)
    query_rows = lax.all_to_all(
        after(targ_normed, enc_partial), "shard", split_axis=1, concat_axis=0, tiled=True
    )
    query_terms = jnp.dot(
        query_rows, dec_qkv(enc_partial)[0], preferred_element_type=jnp.float32
    )
    query_terms = lax.all_to_all(query_terms, "shard", split_axis=0, concat_axis=0, tiled=True)
    targ_accum = jnp.sum(query_terms.reshape(shard_count, -1, head_block), axis=0)
    queries = (targ_accum * scale[pass_rows:, None]).astype(jnp.bfloat16)[None]
    enc_sum = after(enc_sum, queries, *blocks(cross_near))
    encoded = (passage_part.astype(jnp.float32) + enc_sum).astype(jnp.bfloat16)

    whole_encoded = lax.all_gather(encoded, ("mp", "segment"), axis=1, tiled=True)
    cross_far = far(cross_near)
    late_near = near(dec_out(*blocks(cross_far), queries))
    whole_encoded = after(whole_encoded, *blocks(cross_far))
    enc_f32 = whole_encoded.astype(jnp.float32)
    enc_scale = lax.rsqrt(jnp.sum(enc_f32 * enc_f32, axis=1) / D + epsilon)
    enc_normed = (enc_f32 * norm_gains[2]).astype(jnp.bfloat16)
    cross_accum = project(enc_normed, cross_near + cross_far, shard_rows)
    late_far = far([(o, f, after(b, cross_accum)) for o, f, b in late_near])
    key_values = (cross_accum * enc_scale[:, None, None]).astype(jnp.bfloat16)
    dec_context = attend(queries, key_values[None, :, 0], key_values[None, :, 1], head_count)
    dec_partial = lax.dot_general(
        dec_context,
        in_order(late_near + late_far, shard_rows),
        (((1,), (1,)), ((), ())),
        preferred_element_type=jnp.float32,
    ).astype(jnp.bfloat16)
    terms = lax.all_to_all(
        dec_partial, ("mp", "segment"), split_axis=1, concat_axis=0, tiled=True
    )
    terms = terms.reshape(-1, target_part.shape[0], target_part.shape[1]).astype(jnp.float32)
    decoded = (target_part.astype(jnp.float32) + jnp.sum(terms, axis=0)).astype(jnp.bfloat16)
    return (encoded, decoded)


def solution(mesh):
    placed = (
        P("shard", None),
        P(),
        P(),
        P("shard", None),
        P(None, ("mp", "segment")),
        P(),
        P("segment", None, "shard", "mp"),
    )
    return jax.shard_map(
        body,
        mesh=mesh,
        in_specs=placed,
        out_specs=(P("shard", ("mp", "segment")), P("shard", ("mp", "segment"))),
        check_vma=False,
    )
```
